32 devices in a mesh: seq: 8 (over y, x, core), tp: 4 (over z).
Axes of the slice: x: 2, y: 2, z: 4, core: 2. Of those that a mesh axis runs over, the one named last changes fastest.
Arguments:
- grad_out: bfloat16 [1024, 8192], P('seq', 'tp'), may hold values from -6 to 6
- resid_in: bfloat16 [1024, 8192], P('seq', 'tp'), may hold values from -6 to 6
- down_weight: bfloat16 [28672, 8192], P('seq', 'tp'), may hold values from -0.03125 to 0.03125
- hidden_clean: bfloat16 [28672, 512], P('seq', 'tp'), may hold values from -6 to 6
- hidden_corrupt: bfloat16 [28672, 512], P('seq', 'tp'), may hold values from -6 to 6
- patched: int32 [14336], replicated, may hold values from 0 to 28671, as said below
Outputs:
- resid_scores: float32 [1024], P('seq')
- token_scores: float32 [512], P('tp')
- neuron_scores: float32 [28672], P('seq')
The draws below stay inside these ranges and needn't reach their ends.
Inputs may be any that keep to these rules, and one draw needn't show every extreme that they name: `patched`: 14336 distinct hidden-unit indices.
All inputs are finite; a program needn't handle non-finite values.
Results may differ from the reference program's by a relative error of at most 0.0046.
Values may be sent and summed in bfloat16 or wider, within the bound.
A program may use at most 128 MiB of HBM per device.

```python
import math
import jax
import jax.numpy as jnp
from jax import lax

D = 8192
FF = 28672
LEN = 512
NPATCH = 14336


def draw_patched(key, part):
    order = jax.random.permutation(key, FF)
    return order[:NPATCH].astype(jnp.int32)


def levels(key, extent, shards, least, high):
    loudness = 1.0
    for position, shards_of in shards:
        steps = jax.random.uniform(jax.random.fold_in(jax.random.fold_in(key, 6), position), (shards_of,), jnp.float32, least / len(shards), high / len(shards))
        loudness = loudness * jnp.repeat(jnp.exp(steps), extent[position] // shards_of).reshape((-1,) + (1,) * (len(extent) - 1 - position))
    return loudness


def noise(stream_key, extent, scale, bound, pieces=(), held_as=jnp.bfloat16):
    entries = jax.random.normal(stream_key, extent, jnp.float32) * scale
    if len(pieces) > 0:
        entries = levels(stream_key, extent, pieces, -0.22, 0.18) * entries
    return jnp.clip(entries, min=-bound, max=bound).astype(held_as)


def setup_inputs(seed: int = 0) -> dict:
    arg_keys = jax.random.split(jax.random.key(seed), 7)
    return {
        "grad_out": noise(arg_keys[0], (2 * LEN, D), 1.0, 6.0, ((0, 8), (1, 4))),
        "resid_in": noise(arg_keys[1], (2 * LEN, D), 1.0, 6.0, ((0, 8), (1, 4))),
        "down_weight": noise(arg_keys[2], (FF, D), FF ** -0.5, 0.03125, ((0, 8), (1, 4))),
        "hidden_clean": noise(arg_keys[3], (FF, LEN), 1.0, 6.0, ((0, 8), (1, 4))),
        "hidden_corrupt": noise(arg_keys[4], (FF, LEN), 1.0, 6.0, ((0, 8), (1, 4))),
        "patched": draw_patched(jax.random.fold_in(arg_keys[6], 71), 0),
    }


def reference(grad_out, resid_in, down_weight, hidden_clean, hidden_corrupt, patched):
    seq_len = resid_in.shape[0] // 2
    resid_full = resid_in.astype(jnp.float32)
    grad_full = grad_out.astype(jnp.float32)
    resid_diff = resid_full[:seq_len] - resid_full[seq_len:]
    clean_part = lax.optimization_barrier(jnp.sum(resid_diff * grad_full[:seq_len], axis=1))
    corrupt_part = lax.optimization_barrier(jnp.sum(resid_diff * grad_full[seq_len:], axis=1))
    resid_scores = jnp.concatenate([clean_part, corrupt_part]) / math.sqrt(D)
    grad_mean = ((grad_full[:seq_len] + grad_full[seq_len:]) * 0.5).astype(jnp.bfloat16)
    unit_grad = lax.dot_general(down_weight, grad_mean, (((1,), (1,)), ((), ())), preferred_element_type=jnp.float32)
    hidden_diff = (hidden_clean.astype(jnp.float32) - hidden_corrupt.astype(jnp.float32)).astype(jnp.bfloat16)
    product = hidden_diff.astype(jnp.float32) * unit_grad
    in_patch = jnp.zeros((FF,), jnp.float32).at[patched].set(1.0)
    token_scores = lax.optimization_barrier(jnp.sum(product * in_patch[:, None], axis=0)) / math.sqrt(NPATCH)
    neuron_scores = lax.optimization_barrier(jnp.sum(product, axis=1)) / math.sqrt(seq_len)
    return (resid_scores, token_scores, neuron_scores)
```

```python
import math

import jax
import jax.numpy as jnp
from jax import lax
from jax.sharding import PartitionSpec as P


def from_behind(value, axis, steps):
    count = lax.axis_size(axis)
    pairs = [(source, (source + steps) % count) for source in range(count)]
    return lax.ppermute(value, axis, pairs)


def patch_mask(patched, unit_rows):
    lanes = math.gcd(unit_rows, 128)
    groups = unit_rows // lanes
    local = patched - lax.axis_index("seq") * unit_rows
    high = (local[None, :] // lanes) == jnp.arange(groups, dtype=jnp.int32)[:, None]
    high = high & (local >= 0)[None, :]
    low = (local % lanes)[:, None] == jnp.arange(lanes, dtype=jnp.int32)[None, :]
    counts = lax.dot_general(
        high.astype(jnp.bfloat16),
        low.astype(jnp.bfloat16),
        (((1,), (0,)), ((), ())),
        preferred_element_type=jnp.float32,
    )
    return counts.reshape(unit_rows)


def shards(grad_out, resid_in, down_weight, hidden_clean, hidden_corrupt, patched):
    seq_count = lax.axis_size("seq")
    tp_count = lax.axis_size("tp")
    pair_count = seq_count // 2
    half_rows = grad_out.shape[0] // 2
    unit_rows = down_weight.shape[0]
    model_width = resid_in.shape[1] * tp_count
    hidden_diff = (hidden_clean.astype(jnp.float32) - hidden_corrupt.astype(jnp.float32)).astype(
        jnp.bfloat16
    )
    diff_all = lax.all_gather(hidden_diff, "tp", axis=0)
    in_upper = lax.axis_index("seq") // pair_count
    send_start = (1 - in_upper) * half_rows
    keep_start = in_upper * half_rows
    sent_grad = lax.dynamic_slice_in_dim(grad_out, send_start, half_rows, 0)
    partner_grad = from_behind(sent_grad, "seq", pair_count)
    partner_resid = from_behind(resid_in, "seq", pair_count)
    sign_factor = (1 - 2 * in_upper).astype(jnp.float32)
    resid_diff = sign_factor * (resid_in.astype(jnp.float32) - partner_resid.astype(jnp.float32))
    resid_part = jnp.sum(resid_diff * grad_out.astype(jnp.float32), axis=1)
    kept_grad = lax.dynamic_slice_in_dim(grad_out, keep_start, half_rows, 0)
    grad_mean = ((kept_grad.astype(jnp.float32) + partner_grad.astype(jnp.float32)) * 0.5).astype(
        jnp.bfloat16
    )
    grads = lax.all_gather(grad_mean, "seq", axis=0)
    width = grads.shape[-1]
    grads = grads.reshape(2, pair_count, half_rows, width).transpose(1, 0, 2, 3)
    grads = grads.reshape(-1, width)
    total_len = grads.shape[0]
    in_patch = patch_mask(patched, unit_rows)
    unit_grad = lax.dot_general(
        down_weight, grads, (((1,), (1,)), ((), ())), preferred_element_type=jnp.float32
    )
    local_len = total_len // tp_count
    token_parts = []
    unit_part = 0.0
    for block in range(tp_count):
        part = unit_grad[:, block * local_len : (block + 1) * local_len]
        product = diff_all[block].astype(jnp.float32) * part
        token_parts.append(jnp.sum(product * in_patch[:, None], axis=0))
        unit_part = unit_part + jnp.sum(product, axis=1)
    token_part = jnp.stack(token_parts)
    token_total = lax.psum(token_part, ("seq", "tp"))
    token_mine = lax.dynamic_index_in_dim(token_total, lax.axis_index("tp"), 0, keepdims=False)
    token_scores = token_mine / math.sqrt(patched.shape[0])
    unit_total, resid_total = lax.psum((unit_part, resid_part), "tp")
    neuron_scores = unit_total / math.sqrt(total_len)
    resid_scores = resid_total / math.sqrt(model_width)
    return (resid_scores, token_scores, neuron_scores)


def solution(mesh):
    in_specs = (P("seq", "tp"), P("seq", "tp"), P("seq", "tp"), P("seq", "tp"), P("seq", "tp"), P())
    out_specs = (P("seq"), P("tp"), P("seq"))
    return jax.shard_map(shards, mesh=mesh, in_specs=in_specs, out_specs=out_specs, check_vma=False)
```

```python
import functools
import math

import jax
import jax.numpy as jnp
from jax import lax
from jax.experimental import pallas as pl
from jax.experimental.pallas import tpu as pltpu
from jax.sharding import PartitionSpec as P

F32 = jnp.float32
BF16 = jnp.bfloat16
NT = (((1,), (1,)), ((), ()))


def each(count, body):
    def step(index, carry):
        body(index)
        return carry

    lax.fori_loop(0, count, step, 0)


def kernel(
    S, T, C, G, L, R, scales,
    grad_hbm, resid_hbm, weight_hbm, clean_hbm, corrupt_hbm, patched_hbm,
    resid_out, token_out, neuron_out,
    grad, resid, weight, clean, corrupt, patched,
    partner_grad, partner_resid, means, diff, unit, mask, acc, token, token_in, token_sum,
    total_in, message, message_in, counts,
    load_sem, weight_sem, pair_send, pair_recv, mean_send, mean_recv, diff_send, diff_recv,
    msg_send, msg_recv, tok_send, tok_recv, sum_send, sum_recv,
):
    seq = lax.axis_index("seq")
    tp = lax.axis_index("tp")
    pairs = S // 2
    partner = lax.rem(seq + pairs, S)
    upper = seq // pairs
    rows = grad.shape[0]
    half = rows // 2
    units = weight.shape[0]
    piece = units // C
    local_len = diff.shape[2]

    def local(source, target, index):
        return pltpu.make_async_copy(source, target, load_sem.at[index])

    loads = [
        local(clean_hbm, clean, 0),
        local(corrupt_hbm, corrupt, 1),
        local(grad_hbm, grad, 2),
        local(resid_hbm, resid, 3),
        local(patched_hbm, patched, 4),
    ]
    for load in loads:
        load.start()

    def piece_rows(c):
        return pl.ds(pl.multiple_of(c * piece, 16), piece)

    def weight_load(c):
        return pltpu.make_async_copy(
            weight_hbm.at[piece_rows(c)], weight.at[piece_rows(c)], weight_sem.at[c]
        )

    def remote(source, target, send, recv, device):
        return pltpu.make_async_remote_copy(
            src_ref=source, dst_ref=target, send_sem=send, recv_sem=recv,
            device_id=device, device_id_type=pl.DeviceIdType.MESH,
        )

    barrier = pltpu.get_barrier_semaphore()

    def greet_seq(i):
        pl.semaphore_signal(
            barrier, inc=1, device_id=(lax.rem(seq + i + 1, S), tp),
            device_id_type=pl.DeviceIdType.MESH,
        )

    def greet_tp(i):
        pl.semaphore_signal(
            barrier, inc=1, device_id=(seq, lax.rem(tp + i + 1, T)),
            device_id_type=pl.DeviceIdType.MESH,
        )

    each(S - 1, greet_seq)
    each(T - 1, greet_tp)
    loads[0].wait()
    loads[1].wait()

    def subtract(c):
        r = piece_rows(c)
        diff[tp, r, :] = (clean[r, :].astype(F32) - corrupt[r, :].astype(F32)).astype(BF16)

    each(C, subtract)
    loads[2].wait()
    loads[3].wait()
    pl.semaphore_wait(barrier, S - 1 + T - 1)

    send_start = pl.multiple_of((1 - upper) * half, 8)
    keep_start = pl.multiple_of(upper * half, 8)
    grad_copy = remote(
        grad.at[pl.ds(send_start, half)], partner_grad, pair_send.at[0], pair_recv.at[0],
        (partner, tp),
    )
    resid_copy = remote(resid, partner_resid, pair_send.at[1], pair_recv.at[1], (partner, tp))
    grad_copy.start()

    def diff_copy(block, c, step):
        place = diff.at[block, piece_rows(c)]
        direction = (step + 1) // 2
        return remote(
            place, place, diff_send.at[direction, block, c], diff_recv.at[block, c],
            (seq, tp + step),
        )

    def forward(block, c, step):
        @pl.when((tp + step >= 0) & (tp + step < T))
        def _():
            diff_copy(block, c, step).start()

    def own(c):
        forward(tp, c, 1)
        forward(tp, c, -1)

    each(C, own)

    def relay(s, c):
        @pl.when(tp - s >= 0)
        def _():
            diff_copy(tp - s, c, 1).wait_recv()
            forward(tp - s, c, 1)

        @pl.when(tp + s < T)
        def _():
            diff_copy(tp + s, c, -1).wait_recv()
            forward(tp + s, c, -1)

    each(C, lambda c: weight_load(c).start())

    grad_copy.wait()
    slot = lax.rem(seq, pairs) * 2 + upper
    kept = grad[pl.ds(keep_start, half), :].astype(F32)
    means[slot] = ((kept + partner_grad[...].astype(F32)) * 0.5).astype(BF16)

    def mean_copy(i):
        return remote(
            means.at[slot], means.at[slot], mean_send.at[i], mean_recv.at[slot],
            (lax.rem(seq + i, S), tp),
        )

    each(S - 1, lambda i: mean_copy(i + 1).start())
    resid_copy.start()

    loads[4].wait()
    counts[...] = jnp.zeros_like(counts)
    width = patched.shape[1]
    group_ids = lax.broadcasted_iota(jnp.int32, (G, width), 0)
    lane_ids = lax.broadcasted_iota(jnp.int32, (L, width), 0)

    def count(k):
        ids = patched[pl.ds(k, 1), :] - seq * units + S * units
        high = ids // L - (S * units) // L
        low = lax.rem(ids, L)
        counts[...] += lax.dot_general(
            jnp.where(high == group_ids, 1.0, 0.0).astype(BF16),
            jnp.where(low == lane_ids, 1.0, 0.0).astype(BF16),
            NT, preferred_element_type=F32,
        )

    each(patched.shape[0], count)

    def spread(g):
        row = jnp.broadcast_to(counts[pl.ds(g, 1), :], (128, L))
        mask[pl.ds(pl.multiple_of(g * L, 8), L), :] = row.T

    each(G, spread)
    acc[...] = jnp.zeros_like(acc)
    token[...] = jnp.zeros_like(token)

    each(C, lambda c: relay(1, c))

    def await_mean(i):
        source = lax.rem(seq + i + 1, S)
        place = means.at[lax.rem(source, pairs) * 2 + source // pairs]
        sem = mean_recv.at[lax.rem(source, pairs) * 2 + source // pairs]
        remote(place, place, mean_send.at[0], sem, (source, tp)).wait_recv()

    each(S - 1, await_mean)

    def multiply(c):
        weight_load(c).wait()
        r = piece_rows(c)
        left = weight[r, :]
        block_slots = 2 * pairs // T
        for b in range(T):
            right = means[b * block_slots : (b + 1) * block_slots]
            right = right.reshape(local_len, right.shape[-1])
            unit[b, r, :] = lax.dot_general(left, right, NT, preferred_element_type=F32)
        relay(2, c)

    each(C, multiply)

    def product(block, c):
        r = piece_rows(c)
        value = diff[block, r, :].astype(F32) * unit[block, r, :]
        masks = mask[r, :]
        for k in range(local_len // 128):
            part = value[:, k * 128 : (k + 1) * 128]
            acc[r, :] += part
            token[block, :, k * 128 : (k + 1) * 128] += jnp.sum(
                part * masks, axis=0, keepdims=True
            )

    def products(s, c):
        if s == 0:
            product(tp, c)
            return

        @pl.when(tp - s >= 0)
        def _():
            product(tp - s, c)

        @pl.when(tp + s < T)
        def _():
            product(tp + s, c)

    resid_copy.wait()
    sign = (1 - 2 * upper).astype(F32)

    def resid_rows(k):
        r = pl.ds(pl.multiple_of(k * L, 8), L)
        difference = resid[r, :].astype(F32) - partner_resid[r, :].astype(F32)
        terms = sign * difference * grad[r, :].astype(F32)
        folded = terms[:, 0:128]
        for j in range(1, terms.shape[1] // 128):
            folded = folded + terms[:, j * 128 : (j + 1) * 128]
        message[pl.ds(G + k, 1), :] = jnp.sum(folded.T, axis=0, keepdims=True)

    each(R, resid_rows)
    for s in range(min(3, T)):
        each(C, lambda c: products(s, c))
    for s in range(3, T):

        def last(c):
            relay(s, c)
            products(s, c)

        each(C, last)

    def fold(g):
        block = acc[pl.ds(pl.multiple_of(g * L, 8), L), :]
        message[pl.ds(g, 1), :] = jnp.sum(block.T, axis=0, keepdims=True)

    def token_copy(i):
        target = lax.rem(tp + i, T)
        return remote(
            token.at[target], token_in.at[tp], tok_send.at[i], tok_recv.at[tp], (seq, target)
        )

    each(T - 1, lambda i: token_copy(i + 1).start())
    each(G, fold)

    def message_copy(i):
        return remote(
            message, message_in.at[tp], msg_send.at[i], msg_recv.at[tp],
            (seq, lax.rem(tp + i, T)),
        )

    each(T - 1, lambda i: message_copy(i + 1).start())

    token_in[tp] = token[tp]

    def await_token(i):
        source = lax.rem(tp + i + 1, T)
        remote(
            token.at[0], token_in.at[source], tok_send.at[0], tok_recv.at[source], (seq, source)
        ).wait_recv()

    each(T - 1, await_token)
    token_sum[...] = jnp.sum(token_in[...], axis=0)

    def sum_copy(i):
        return remote(
            token_sum, total_in.at[seq], sum_send.at[i], sum_recv.at[seq],
            (lax.rem(seq + i, S), tp),
        )

    each(S - 1, lambda i: sum_copy(i + 1).start())
    total_in[seq] = token_sum[...]
    message_in[tp] = message[...]

    def await_message(i):
        source = lax.rem(tp + i + 1, T)
        remote(
            message, message_in.at[source], msg_send.at[0], msg_recv.at[source], (seq, source)
        ).wait_recv()

    each(T - 1, await_message)
    total = jnp.sum(message_in[...], axis=0)
    neuron_out[...] = total[:G] * scales[2]
    resid_out[...] = total[G:] * scales[0]

    def await_sum(i):
        source = lax.rem(seq + i + 1, S)
        remote(
            token_sum, total_in.at[source], sum_send.at[0], sum_recv.at[source], (source, tp)
        ).wait_recv()

    each(S - 1, await_sum)
    token_out[...] = jnp.sum(total_in[...], axis=0) * scales[1]

    each(S - 1, lambda i: mean_copy(i + 1).wait_send())
    each(T - 1, lambda i: token_copy(i + 1).wait_send())
    each(T - 1, lambda i: message_copy(i + 1).wait_send())
    each(S - 1, lambda i: sum_copy(i + 1).wait_send())

    def drain(c):
        def sent(block, step):
            @pl.when((tp + step >= 0) & (tp + step < T) & (block >= 0) & (block < T))
            def _():
                diff_copy(block, c, step).wait_send()

        for s in range(T):
            sent(tp - s, 1)
            sent(tp + s, -1)

    each(C, drain)


def shards(grad_out, resid_in, down_weight, hidden_clean, hidden_corrupt, patched):
    S = lax.axis_size("seq")
    T = lax.axis_size("tp")
    rows, width = grad_out.shape
    units, local_len = hidden_clean.shape
    C = max(c for c in range(1, 9) if units % (16 * c) == 0)
    L = math.gcd(units, 128)
    G = units // L
    R = rows // L
    lanes = math.gcd(patched.shape[0], 1024)
    half = rows // 2
    scales = (
        1.0 / math.sqrt(width * T),
        1.0 / math.sqrt(patched.shape[0]),
        1.0 / math.sqrt(local_len * T),
    )
    dma = lambda *shape: pltpu.SemaphoreType.DMA(shape)
    resid, token, neuron = pl.pallas_call(
        functools.partial(kernel, S, T, C, G, L, R, scales),
        out_shape=(
            jax.ShapeDtypeStruct((R, L), F32),
            jax.ShapeDtypeStruct((1, local_len), F32),
            jax.ShapeDtypeStruct((G, L), F32),
        ),
        in_specs=[pl.BlockSpec(memory_space=pl.ANY)] * 6,
        out_specs=[pl.BlockSpec(memory_space=pltpu.VMEM)] * 3,
        scratch_shapes=[
            pltpu.VMEM((rows, width), BF16),
            pltpu.VMEM((rows, width), BF16),
            pltpu.VMEM((units, width), BF16),
            pltpu.VMEM((units, local_len), BF16),
            pltpu.VMEM((units, local_len), BF16),
            pltpu.VMEM((patched.shape[0] // lanes, lanes), jnp.int32),
            pltpu.VMEM((half, width), BF16),
            pltpu.VMEM((rows, width), BF16),
            pltpu.VMEM((S, half, width), BF16),
            pltpu.VMEM((T, units, local_len), BF16),
            pltpu.VMEM((T, units, local_len), F32),
            pltpu.VMEM((units, 128), F32),
            pltpu.VMEM((units, 128), F32),
            pltpu.VMEM((T, 1, local_len), F32),
            pltpu.VMEM((T, 1, local_len), F32),
            pltpu.VMEM((1, local_len), F32),
            pltpu.VMEM((S, 1, local_len), F32),
            pltpu.VMEM((G + R, L), F32),
            pltpu.VMEM((T, G + R, L), F32),
            pltpu.VMEM((G, L), F32),
            dma(5), dma(C), dma(2), dma(2), dma(S), dma(S), dma(2, T, C), dma(T, C),
            dma(T), dma(T), dma(T), dma(T), dma(S), dma(S),
        ],
        compiler_params=pltpu.CompilerParams(
            collective_id=0, has_side_effects=True, vmem_limit_bytes=56 * 1024 * 1024
        ),
    )(
        grad_out, resid_in, down_weight, hidden_clean, hidden_corrupt,
        patched.reshape(-1, lanes),
    )
    return (resid.reshape(rows), token.reshape(local_len), neuron.reshape(units))


def solution(mesh):
    in_specs = (P("seq", "tp"), P("seq", "tp"), P("seq", "tp"), P("seq", "tp"), P("seq", "tp"), P())
    out_specs = (P("seq"), P("tp"), P("seq"))
    return jax.shard_map(shards, mesh=mesh, in_specs=in_specs, out_specs=out_specs, check_vma=False)
```

```python
import functools
import math

import jax
import jax.numpy as jnp
from jax import lax
from jax.experimental import pallas as pl
from jax.experimental.pallas import tpu as pltpu
from jax.sharding import PartitionSpec as P

F32 = jnp.float32
BF16 = jnp.bfloat16
NT = (((1,), (1,)), ((), ()))


def each(count, body):
    def step(index, carry):
        body(index)
        return carry

    lax.fori_loop(0, count, step, 0)


def kernel(
    S, T, C, G, L, scales,
    grad_hbm, resid_hbm, weight_hbm, clean_hbm, corrupt_hbm, patched_hbm,
    resid_out, token_out, neuron_out,
    grad, resid, weight, clean, corrupt, patched,
    partner_grad, partner_resid, means, diff, unit, partial, partial_in, mask, acc, token, token_in, token_sum,
    total_in, message, message_in, counts, scored, score_out,
    load_sem, weight_sem, pair_send, pair_recv, outer_send, inner_send, mean_recv, diff_send, diff_recv,
    part_send, part_recv, msg_send, msg_recv, tok_send, tok_recv, sum_send, sum_recv,
):
    seq = lax.axis_index("seq")
    tp = lax.axis_index("tp")
    pairs = S // 2
    partner = lax.rem(seq + pairs, S)
    upper = seq // pairs
    rows = grad.shape[0]
    half = rows // 2
    units = weight.shape[0]
    piece = units // C
    local_len = diff.shape[2]

    def local(source, target, index):
        return pltpu.make_async_copy(source, target, load_sem.at[index])

    loads = [
        local(clean_hbm, clean, 0),
        local(corrupt_hbm, corrupt, 1),
        local(grad_hbm, grad, 2),
        local(resid_hbm, resid, 3),
        local(patched_hbm, patched, 4),
    ]
    for load in loads:
        load.start()

    def piece_rows(c):
        return pl.ds(pl.multiple_of(c * piece, 16), piece)

    def weight_load(c):
        return pltpu.make_async_copy(
            weight_hbm.at[piece_rows(c)], weight.at[piece_rows(c)], weight_sem.at[c]
        )

    def remote(source, target, send, recv, device):
        return pltpu.make_async_remote_copy(
            src_ref=source, dst_ref=target, send_sem=send, recv_sem=recv,
            device_id=device, device_id_type=pl.DeviceIdType.MESH,
        )

    barrier = pltpu.get_barrier_semaphore()

    def greet_seq(i):
        pl.semaphore_signal(
            barrier, inc=1, device_id=(lax.rem(seq + i + 1, S), tp),
            device_id_type=pl.DeviceIdType.MESH,
        )

    def greet_tp(i):
        pl.semaphore_signal(
            barrier, inc=1, device_id=(seq, lax.rem(tp + i + 1, T)),
            device_id_type=pl.DeviceIdType.MESH,
        )

    each(S - 1, greet_seq)
    each(T - 1, greet_tp)
    loads[0].wait()
    loads[1].wait()

    def subtract(c):
        r = piece_rows(c)
        diff[tp, r, :] = (clean[r, :].astype(F32) - corrupt[r, :].astype(F32)).astype(BF16)

    each(C, subtract)
    loads[2].wait()
    loads[3].wait()
    pl.semaphore_wait(barrier, S - 1 + T - 1)

    keep = pl.ds(pl.multiple_of(upper * half, 8), half)
    give = pl.ds(pl.multiple_of((1 - upper) * half, 8), half)

    def grad_copy(h):
        r = pl.ds(h * half, half)
        return remote(
            grad.at[r], partner_grad.at[r], pair_send.at[h], pair_recv.at[h], (partner, tp)
        )

    resid_copy = remote(
        resid.at[give], partner_resid, pair_send.at[2], pair_recv.at[2], (partner, tp)
    )
    score_copy = remote(
        score_out, scored.at[upper], pair_send.at[3], pair_recv.at[3], (partner, tp)
    )
    grad_copy(0).start()
    grad_copy(1).start()

    def diff_copy(block, c, step):
        place = diff.at[block, piece_rows(c)]
        direction = (step + 1) // 2
        return remote(
            place, place, diff_send.at[direction, block, c], diff_recv.at[block, c],
            (seq, tp + step),
        )

    def forward(block, c, step):
        @pl.when((tp + step >= 0) & (tp + step < T))
        def _():
            diff_copy(block, c, step).start()

    def own(c):
        forward(tp, c, 1)
        forward(tp, c, -1)

    each(C, own)

    def relay(s, c):
        @pl.when(tp - s >= 0)
        def _():
            diff_copy(tp - s, c, 1).wait_recv()
            if s + 1 <= T - 2:
                forward(tp - s, c, 1)

        @pl.when(tp + s < T)
        def _():
            diff_copy(tp + s, c, -1).wait_recv()
            if s + 1 <= T - 2:
                forward(tp + s, c, -1)

    each(C, lambda c: weight_load(c).start())

    outer = pairs // 2
    mine = lax.rem(seq, pairs)
    chip = mine // 2
    core = lax.rem(mine, 2)

    def mean_copy(block, h, send, target):
        place = means.at[block, pl.ds(h * half, half)]
        return remote(place, place, send, mean_recv.at[block, h], (upper * pairs + target, tp))

    def outer_copy(i, h):
        return mean_copy(mine, h, outer_send.at[i, h], lax.rem(chip + i, outer) * 2 + core)

    def inner_copy(i, h):
        block = lax.rem(chip + i, outer) * 2 + core
        return mean_copy(block, h, inner_send.at[i, h], chip * 2 + 1 - core)

    def await_mean(block, h):
        mean_copy(block, h, inner_send.at[0, h], chip * 2 + 1 - core).wait_recv()

    for h in range(2):
        grad_copy(h).wait()
        r = pl.ds(h * half, half)
        both = grad[r, :].astype(F32) + partner_grad[r, :].astype(F32)
        means[mine, r, :] = (both * 0.5).astype(BF16)
        each(outer - 1, lambda i: outer_copy(i + 1, h).start())
        inner_copy(0, h).start()
    resid_copy.start()

    loads[4].wait()
    counts[...] = jnp.zeros_like(counts)
    width = patched.shape[1]
    group_ids = lax.broadcasted_iota(jnp.int32, (G, width), 0)
    lane_ids = lax.broadcasted_iota(jnp.int32, (L, width), 0)

    def count(k):
        ids = patched[pl.ds(k, 1), :] - seq * units + S * units
        high = ids // L - (S * units) // L
        low = lax.rem(ids, L)
        counts[...] += lax.dot_general(
            jnp.where(high == group_ids, 1.0, 0.0).astype(BF16),
            jnp.where(low == lane_ids, 1.0, 0.0).astype(BF16),
            NT, preferred_element_type=F32,
        )

    each(patched.shape[0], count)

    def spread(g):
        row = jnp.broadcast_to(counts[pl.ds(g, 1), :], (128, L))
        mask[pl.ds(pl.multiple_of(g * L, 8), L), :] = row.T

    each(G, spread)
    acc[...] = jnp.zeros_like(acc)
    token[...] = jnp.zeros_like(token)

    each(C // 2, lambda c: relay(1, c))
    for h in range(2):

        def pass_on(i):
            await_mean(lax.rem(chip + i + 1, outer) * 2 + core, h)
            inner_copy(i + 1, h).start()

        each(outer - 1, pass_on)
    each(C - C // 2, lambda c: relay(1, c + C // 2))
    for h in range(2):
        each(outer, lambda i: await_mean(lax.rem(chip + i, outer) * 2 + 1 - core, h))

    blocks = T // 2
    at_end = (tp == 0) | (tp == T - 1)
    far = jnp.where(tp == 0, T - 1, 0)
    inward = jnp.where(tp == 0, 1, -1)

    def partial_copy(c):
        r = piece_rows(c)
        return remote(
            partial.at[r], partial_in.at[r], part_send.at[c], part_recv.at[c], (seq, tp + inward)
        )

    def multiply(side, c):
        r = piece_rows(c)
        right = means[pl.ds(side * outer, outer)]
        right = right.reshape(outer * rows, right.shape[-1])
        result = lax.dot_general(weight[r, :], right, NT, preferred_element_type=F32)
        for k in range(blocks):
            unit[side * blocks + k, r, :] = result[:, k * local_len : (k + 1) * local_len]

    far_side = 1 - tp // blocks

    def multiply_far(c):
        weight_load(c).wait()
        multiply(far_side, c)

        @pl.when(at_end)
        def _():
            r = piece_rows(c)
            partial[r, :] = unit[far, r, :].astype(BF16)
            partial_copy(c).start()

    each(C, multiply_far)
    each(C, lambda c: multiply(1 - far_side, c))

    def product(block, c):
        r = piece_rows(c)
        value = diff[block, r, :].astype(F32) * unit[block, r, :]
        masks = mask[r, :]
        for k in range(local_len // 128):
            part = value[:, k * 128 : (k + 1) * 128]
            acc[r, :] += part
            token[block, :, k * 128 : (k + 1) * 128] += jnp.sum(
                part * masks, axis=0, keepdims=True
            )

    def products(s, c):
        if s == 0:
            product(tp, c)
            return

        @pl.when(tp - s >= 0)
        def _():
            product(tp - s, c)

        @pl.when(tp + s < T)
        def _():
            product(tp + s, c)

    resid_copy.wait()
    sign = (1 - 2 * upper).astype(F32)

    difference = sign * (resid[keep, :].astype(F32) - partner_resid[...].astype(F32))

    def score(gradient):
        terms = difference * gradient.astype(F32)
        folded = terms[:, 0:128]
        for j in range(1, terms.shape[1] // 128):
            folded = folded + terms[:, j * 128 : (j + 1) * 128]
        return jnp.sum(folded.T, axis=0, keepdims=True)

    score_out[...] = score(partner_grad[keep, :])
    score_copy.start()
    scored[upper] = score(grad[keep, :])
    each(C, lambda c: products(0, c))
    each(C, lambda c: products(1, c))
    helped = ((tp == 1) | (tp == T - 2)) & (T > 2)
    helped_block = jnp.where(tp == 1, T - 1, 0)

    def help_in(c):
        @pl.when(helped)
        def _():
            r = piece_rows(c)
            remote(
                partial.at[r], partial_in.at[r], part_send.at[c], part_recv.at[c],
                (seq, jnp.where(tp == 1, 0, T - 1)),
            ).wait_recv()
            unit[helped_block, r, :] += partial_in[r, :].astype(F32)

    for s in range(2, T - 1):

        def last(c):
            relay(s, c)
            if s == T - 2:
                help_in(c)
            products(s, c)

        each(C, last)
    score_copy.wait()
    message[G:, :] = jnp.zeros((2, L), F32)
    for k in range(2):
        message[G + k : G + k + 1, 0:half] = scored[k]

    def fold(g):
        block = acc[pl.ds(pl.multiple_of(g * L, 8), L), :]
        message[pl.ds(g, 1), :] = jnp.sum(block.T, axis=0, keepdims=True)

    def token_copy(i):
        target = lax.rem(tp + i, T)
        return remote(
            token.at[target], token_in.at[tp], tok_send.at[i], tok_recv.at[tp], (seq, target)
        )

    each(T - 1, lambda i: token_copy(i + 1).start())
    each(G, fold)

    def message_copy(i):
        return remote(
            message, message_in.at[tp], msg_send.at[i], msg_recv.at[tp],
            (seq, lax.rem(tp + i, T)),
        )

    each(T - 1, lambda i: message_copy(i + 1).start())

    token_in[tp] = token[tp]

    def await_token(i):
        source = lax.rem(tp + i + 1, T)
        remote(
            token.at[0], token_in.at[source], tok_send.at[0], tok_recv.at[source], (seq, source)
        ).wait_recv()

    each(T - 1, await_token)
    token_sum[...] = jnp.sum(token_in[...], axis=0)

    def sum_copy(i):
        return remote(
            token_sum, total_in.at[seq], sum_send.at[i], sum_recv.at[seq],
            (lax.rem(seq + i, S), tp),
        )

    each(S - 1, lambda i: sum_copy(i + 1).start())
    total_in[seq] = token_sum[...]
    message_in[tp] = message[...]

    def await_message(i):
        source = lax.rem(tp + i + 1, T)
        remote(
            message, message_in.at[source], msg_send.at[0], msg_recv.at[source], (seq, source)
        ).wait_recv()

    each(T - 1, await_message)
    total = jnp.sum(message_in[...], axis=0)
    neuron_out[...] = total[:G] * scales[2]
    resid_out[...] = total[G:, 0:half] * scales[0]

    def await_sum(i):
        source = lax.rem(seq + i + 1, S)
        remote(
            token_sum, total_in.at[source], sum_send.at[0], sum_recv.at[source], (source, tp)
        ).wait_recv()

    each(S - 1, await_sum)
    token_out[...] = jnp.sum(total_in[...], axis=0) * scales[1]

    for h in range(2):
        each(outer - 1, lambda i: outer_copy(i + 1, h).wait_send())
        each(outer, lambda i: inner_copy(i, h).wait_send())
    each(T - 1, lambda i: token_copy(i + 1).wait_send())
    each(T - 1, lambda i: message_copy(i + 1).wait_send())
    each(S - 1, lambda i: sum_copy(i + 1).wait_send())

    def drain(c):
        def sent(block, step):
            @pl.when((tp + step >= 0) & (tp + step < T) & (block >= 0) & (block < T))
            def _():
                diff_copy(block, c, step).wait_send()

        for s in range(T - 2):
            sent(tp - s, 1)
            sent(tp + s, -1)

    each(C, drain)

    @pl.when(at_end)
    def _():
        each(C, lambda c: partial_copy(c).wait_send())


def shards(grad_out, resid_in, down_weight, hidden_clean, hidden_corrupt, patched):
    S = lax.axis_size("seq")
    T = lax.axis_size("tp")
    rows, width = grad_out.shape
    units, local_len = hidden_clean.shape
    C = max(c for c in range(1, 9) if units % (16 * c) == 0)
    L = math.gcd(units, 128)
    G = units // L
    lanes = math.gcd(patched.shape[0], 1024)
    half = rows // 2
    scales = (
        1.0 / math.sqrt(width * T),
        1.0 / math.sqrt(patched.shape[0]),
        1.0 / math.sqrt(local_len * T),
    )
    dma = lambda *shape: pltpu.SemaphoreType.DMA(shape)
    resid, token, neuron = pl.pallas_call(
        functools.partial(kernel, S, T, C, G, L, scales),
        out_shape=(
            jax.ShapeDtypeStruct((2, half), F32),
            jax.ShapeDtypeStruct((1, local_len), F32),
            jax.ShapeDtypeStruct((G, L), F32),
        ),
        in_specs=[pl.BlockSpec(memory_space=pl.ANY)] * 6,
        out_specs=[pl.BlockSpec(memory_space=pltpu.VMEM)] * 3,
        scratch_shapes=[
            pltpu.VMEM((rows, width), BF16),
            pltpu.VMEM((rows, width), BF16),
            pltpu.VMEM((units, width), BF16),
            pltpu.VMEM((units, local_len), BF16),
            pltpu.VMEM((units, local_len), BF16),
            pltpu.VMEM((patched.shape[0] // lanes, lanes), jnp.int32),
            pltpu.VMEM((rows, width), BF16),
            pltpu.VMEM((half, width), BF16),
            pltpu.VMEM((S // 2, rows, width), BF16),
            pltpu.VMEM((T, units, local_len), BF16),
            pltpu.VMEM((T, units, local_len), F32),
            pltpu.VMEM((units, local_len), BF16),
            pltpu.VMEM((units, local_len), BF16),
            pltpu.VMEM((units, 128), F32),
            pltpu.VMEM((units, 128), F32),
            pltpu.VMEM((T, 1, local_len), F32),
            pltpu.VMEM((T, 1, local_len), F32),
            pltpu.VMEM((1, local_len), F32),
            pltpu.VMEM((S, 1, local_len), F32),
            pltpu.VMEM((G + 2, L), F32),
            pltpu.VMEM((T, G + 2, L), F32),
            pltpu.VMEM((G, L), F32),
            pltpu.VMEM((2, 1, half), F32),
            pltpu.VMEM((1, half), F32),
            dma(5), dma(C), dma(4), dma(4), dma(S // 4, 2), dma(S // 4, 2), dma(S // 2, 2),
            dma(2, T, C), dma(T, C), dma(C), dma(C),
            dma(T), dma(T), dma(T), dma(T), dma(S), dma(S),
        ],
        compiler_params=pltpu.CompilerParams(
            collective_id=0, has_side_effects=True, vmem_limit_bytes=56 * 1024 * 1024
        ),
    )(
        grad_out, resid_in, down_weight, hidden_clean, hidden_corrupt,
        patched.reshape(-1, lanes),
    )
    return (resid.reshape(rows), token.reshape(local_len), neuron.reshape(units))


def solution(mesh):
    in_specs = (P("seq", "tp"), P("seq", "tp"), P("seq", "tp"), P("seq", "tp"), P("seq", "tp"), P())
    out_specs = (P("seq"), P("tp"), P("seq"))
    return jax.shard_map(shards, mesh=mesh, in_specs=in_specs, out_specs=out_specs, check_vma=False)
```

```python
import functools
import math

import jax
import jax.numpy as jnp
from jax import lax
from jax.experimental import pallas as pl
from jax.experimental.pallas import tpu as pltpu
from jax.sharding import PartitionSpec as P

F32 = jnp.float32
BF16 = jnp.bfloat16
NT = (((1,), (1,)), ((), ()))


def each(count, body):
    def step(index, carry):
        body(index)
        return carry

    lax.fori_loop(0, count, step, 0)


def kernel(
    S, T, C, G, L, scales,
    grad_hbm, resid_hbm, weight_hbm, clean_hbm, corrupt_hbm, patched_hbm,
    scores,
    grad, resid, weight, clean, corrupt, patched,
    partner_grad, partner_resid, means, diff, unit, partial, partial_in, mask, acc, token, token_in, token_sum,
    total_in, message, message_in, counts, scored, score_out,
    load_sem, weight_sem, pair_send, pair_recv, outer_send, inner_send, mean_recv, diff_send, diff_recv,
    part_send, part_recv, msg_send, msg_recv, tok_send, tok_recv, sum_send, sum_recv,
):
    seq = lax.axis_index("seq")
    tp = lax.axis_index("tp")
    pairs = S // 2
    partner = lax.rem(seq + pairs, S)
    upper = seq // pairs
    rows = grad.shape[0]
    half = rows // 2
    units = weight.shape[0]
    piece = units // C
    local_len = diff.shape[2]

    lanes = patched.shape[2]

    def local(source, target, index):
        return pltpu.make_async_copy(source, target, load_sem.at[index])

    loads = [
        local(clean_hbm, clean, 0),
        local(corrupt_hbm, corrupt, 1),
        local(grad_hbm, grad, 2),
        local(resid_hbm, resid, 3),
    ]
    for index in (2, 0, 1, 3):
        loads[index].start()

    def ids_load(k):
        return local(patched_hbm.at[pl.ds(pl.multiple_of(k * lanes, lanes), lanes)], patched.at[k, 0], 4 + k)

    each(patched.shape[0], lambda k: ids_load(k).start())

    def piece_rows(c):
        return pl.ds(pl.multiple_of(c * piece, 16), piece)

    def weight_load(c):
        return pltpu.make_async_copy(
            weight_hbm.at[piece_rows(c)], weight.at[piece_rows(c)], weight_sem.at[c]
        )

    def remote(source, target, send, recv, device):
        return pltpu.make_async_remote_copy(
            src_ref=source, dst_ref=target, send_sem=send, recv_sem=recv,
            device_id=device, device_id_type=pl.DeviceIdType.MESH,
        )

    barrier = pltpu.get_barrier_semaphore()

    def greet_seq(i):
        pl.semaphore_signal(
            barrier, inc=1, device_id=(lax.rem(seq + i + 1, S), tp),
            device_id_type=pl.DeviceIdType.MESH,
        )

    def greet_tp(i):
        pl.semaphore_signal(
            barrier, inc=1, device_id=(seq, lax.rem(tp + i + 1, T)),
            device_id_type=pl.DeviceIdType.MESH,
        )

    each(S - 1, greet_seq)
    each(T - 1, greet_tp)
    loads[2].wait()
    pl.semaphore_wait(barrier, S - 1 + T - 1)
    keep = pl.ds(pl.multiple_of(upper * half, 8), half)
    give = pl.ds(pl.multiple_of((1 - upper) * half, 8), half)

    def grad_copy(h):
        r = pl.ds(h * half, half)
        return remote(
            grad.at[r], partner_grad.at[r], pair_send.at[h], pair_recv.at[h], (partner, tp)
        )

    resid_copy = remote(
        resid.at[give], partner_resid, pair_send.at[2], pair_recv.at[2], (partner, tp)
    )
    score_copy = remote(
        score_out, scored.at[upper], pair_send.at[3], pair_recv.at[3], (partner, tp)
    )
    grad_copy(0).start()
    grad_copy(1).start()

    def diff_copy(block, c, step):
        place = diff.at[block, piece_rows(c)]
        direction = (step + 1) // 2
        return remote(
            place, place, diff_send.at[direction, block, c], diff_recv.at[block, c],
            (seq, tp + step),
        )

    def forward(block, c, step):
        @pl.when((tp + step >= 0) & (tp + step < T))
        def _():
            diff_copy(block, c, step).start()

    def own(c):
        forward(tp, c, 1)
        forward(tp, c, -1)

    loads[0].wait()
    loads[1].wait()

    def subtract(c):
        r = piece_rows(c)
        diff[tp, r, :] = (clean[r, :].astype(F32) - corrupt[r, :].astype(F32)).astype(BF16)
        own(c)

    each(C, subtract)

    def relay(s, c):
        @pl.when(tp - s >= 0)
        def _():
            diff_copy(tp - s, c, 1).wait_recv()
            if s + 1 <= T - 2:
                forward(tp - s, c, 1)

        @pl.when(tp + s < T)
        def _():
            diff_copy(tp + s, c, -1).wait_recv()
            if s + 1 <= T - 2:
                forward(tp + s, c, -1)

    each(C, lambda c: weight_load(c).start())

    outer = pairs // 2
    mine = lax.rem(seq, pairs)
    chip = mine // 2
    core = lax.rem(mine, 2)

    def mean_copy(block, h, send, target):
        place = means.at[block, pl.ds(h * half, half)]
        return remote(place, place, send, mean_recv.at[block, h], (upper * pairs + target, tp))

    def outer_copy(i, h):
        return mean_copy(mine, h, outer_send.at[i, h], lax.rem(chip + i, outer) * 2 + core)

    def inner_copy(i, h):
        block = lax.rem(chip + i, outer) * 2 + core
        return mean_copy(block, h, inner_send.at[i, h], chip * 2 + 1 - core)

    def await_mean(block, h):
        mean_copy(block, h, inner_send.at[0, h], chip * 2 + 1 - core).wait_recv()

    for h in range(2):
        grad_copy(h).wait()
        r = pl.ds(h * half, half)
        both = grad[r, :].astype(F32) + partner_grad[r, :].astype(F32)
        means[mine, r, :] = (both * 0.5).astype(BF16)
        each(outer - 1, lambda i: outer_copy(i + 1, h).start())
        inner_copy(0, h).start()
    loads[3].wait()
    resid_copy.start()

    each(patched.shape[0], lambda k: ids_load(k).wait())
    counts[...] = jnp.zeros_like(counts)
    group_ids = lax.broadcasted_iota(jnp.int32, (G, lanes), 0)
    lane_ids = lax.broadcasted_iota(jnp.int32, (L, lanes), 0)

    def count(k):
        ids = patched[k] - seq * units + S * units
        high = ids // L - (S * units) // L
        low = lax.rem(ids, L)
        counts[...] += lax.dot_general(
            jnp.where(high == group_ids, 1.0, 0.0).astype(BF16),
            jnp.where(low == lane_ids, 1.0, 0.0).astype(BF16),
            NT, preferred_element_type=F32,
        )

    each(patched.shape[0], count)

    def spread(g):
        row = jnp.broadcast_to(counts[pl.ds(g, 1), :], (128, L))
        mask[pl.ds(pl.multiple_of(g * L, 8), L), :] = row.T

    each(G, spread)
    acc[...] = jnp.zeros_like(acc)
    token[...] = jnp.zeros_like(token)

    each(C // 2, lambda c: relay(1, c))
    for h in range(2):

        def pass_on(i):
            await_mean(lax.rem(chip + i + 1, outer) * 2 + core, h)
            inner_copy(i + 1, h).start()

        each(outer - 1, pass_on)
    each(C - C // 2, lambda c: relay(1, c + C // 2))
    for h in range(2):
        each(outer, lambda i: await_mean(lax.rem(chip + i, outer) * 2 + 1 - core, h))

    blocks = T // 2
    at_end = (tp == 0) | (tp == T - 1)
    far = jnp.where(tp == 0, T - 1, 0)
    inward = jnp.where(tp == 0, 1, -1)

    def partial_copy(c):
        r = piece_rows(c)
        return remote(
            partial.at[r], partial_in.at[r], part_send.at[c], part_recv.at[c], (seq, tp + inward)
        )

    def multiply(side, c):
        r = piece_rows(c)
        right = means[pl.ds(side * outer, outer)]
        right = right.reshape(outer * rows, right.shape[-1])
        result = lax.dot_general(weight[r, :], right, NT, preferred_element_type=F32)
        for k in range(blocks):
            unit[side * blocks + k, r, :] = result[:, k * local_len : (k + 1) * local_len]

    far_side = 1 - tp // blocks

    def multiply_far(c):
        weight_load(c).wait()
        multiply(far_side, c)

        @pl.when(at_end)
        def _():
            r = piece_rows(c)
            partial[r, :] = unit[far, r, :].astype(BF16)
            partial_copy(c).start()

    each(C, multiply_far)
    each(C, lambda c: multiply(1 - far_side, c))

    def product(block, c):
        r = piece_rows(c)
        value = diff[block, r, :].astype(F32) * unit[block, r, :]
        masks = mask[r, :]
        for k in range(local_len // 128):
            part = value[:, k * 128 : (k + 1) * 128]
            acc[r, :] += part
            token[block, :, k * 128 : (k + 1) * 128] += jnp.sum(
                part * masks, axis=0, keepdims=True
            )

    def products(s, c):
        if s == 0:
            product(tp, c)
            return

        @pl.when(tp - s >= 0)
        def _():
            product(tp - s, c)

        @pl.when(tp + s < T)
        def _():
            product(tp + s, c)

    resid_copy.wait()
    sign = (1 - 2 * upper).astype(F32)

    difference = sign * (resid[keep, :].astype(F32) - partner_resid[...].astype(F32))

    def score(gradient):
        terms = difference * gradient.astype(F32)
        folded = terms[:, 0:128]
        for j in range(1, terms.shape[1] // 128):
            folded = folded + terms[:, j * 128 : (j + 1) * 128]
        return jnp.sum(folded.T, axis=0, keepdims=True)

    score_out[...] = score(partner_grad[keep, :])
    score_copy.start()
    scored[upper] = score(grad[keep, :])
    each(C, lambda c: products(0, c))
    each(C, lambda c: products(1, c))
    helped = ((tp == 1) | (tp == T - 2)) & (T > 2)
    helped_block = jnp.where(tp == 1, T - 1, 0)

    def help_in(c):
        @pl.when(helped)
        def _():
            r = piece_rows(c)
            remote(
                partial.at[r], partial_in.at[r], part_send.at[c], part_recv.at[c],
                (seq, jnp.where(tp == 1, 0, T - 1)),
            ).wait_recv()
            unit[helped_block, r, :] += partial_in[r, :].astype(F32)

    def fold(g):
        block = acc[pl.ds(pl.multiple_of(g * L, 8), L), :]
        message[pl.ds(g, 1), :] = jnp.sum(block.T, axis=0, keepdims=True)

    score_copy.wait()
    message[G:, :] = jnp.zeros((2, L), F32)
    for k in range(2):
        message[G + k : G + k + 1, 0:half] = scored[k]

    for s in range(2, T - 1):

        def last(c):
            relay(s, c)
            if s == T - 2:
                help_in(c)
            products(s, c)
            if s == T - 2:
                each(G // C, lambda g: fold(c * (G // C) + g))

        each(C, last)
    def token_copy(i):
        target = lax.rem(tp + i, T)
        return remote(
            token.at[target], token_in.at[tp], tok_send.at[i], tok_recv.at[tp], (seq, target)
        )

    each(T - 1, lambda i: token_copy(i + 1).start())

    def message_copy(i):
        return remote(
            message, message_in.at[tp], msg_send.at[i], msg_recv.at[tp],
            (seq, lax.rem(tp + i, T)),
        )

    each(T - 1, lambda i: message_copy(i + 1).start())

    token_in[tp] = token[tp]
    for h in range(2):
        each(outer - 1, lambda i: outer_copy(i + 1, h).wait_send())
        each(outer, lambda i: inner_copy(i, h).wait_send())

    def drain(c):
        def sent(block, step):
            @pl.when((tp + step >= 0) & (tp + step < T) & (block >= 0) & (block < T))
            def _():
                diff_copy(block, c, step).wait_send()

        for s in range(T - 2):
            sent(tp - s, 1)
            sent(tp + s, -1)

    each(C, drain)

    @pl.when(at_end)
    def _():
        each(C, lambda c: partial_copy(c).wait_send())

    def await_token(i):
        source = lax.rem(tp + i + 1, T)
        remote(
            token.at[0], token_in.at[source], tok_send.at[0], tok_recv.at[source], (seq, source)
        ).wait_recv()

    each(T - 1, await_token)
    token_sum[...] = jnp.sum(token_in[...], axis=0)

    def sum_copy(i):
        return remote(
            token_sum, total_in.at[seq], sum_send.at[i], sum_recv.at[seq],
            (lax.rem(seq + i, S), tp),
        )

    each(S - 1, lambda i: sum_copy(i + 1).start())
    total_in[seq] = token_sum[...]
    message_in[tp] = message[...]

    def await_message(i):
        source = lax.rem(tp + i + 1, T)
        remote(
            message, message_in.at[source], msg_send.at[0], msg_recv.at[source], (seq, source)
        ).wait_recv()

    each(T - 1, await_message)
    total = jnp.sum(message_in[...], axis=0)
    scores[0:G, :] = total[:G] * scales[2]
    scores[G : G + 2, :] = total[G:] * scales[0]

    def await_sum(i):
        source = lax.rem(seq + i + 1, S)
        remote(
            token_sum, total_in.at[source], sum_send.at[0], sum_recv.at[source], (source, tp)
        ).wait_recv()

    each(S - 1, await_sum)
    token_total = jnp.sum(total_in[...], axis=0) * scales[1]
    for k in range(local_len // L):
        scores[G + 2 + k : G + 3 + k, :] = token_total[:, k * L : (k + 1) * L]

    each(T - 1, lambda i: token_copy(i + 1).wait_send())
    each(T - 1, lambda i: message_copy(i + 1).wait_send())
    each(S - 1, lambda i: sum_copy(i + 1).wait_send())


def write(G, K, L, half, scores, resid_out, token_out, neuron_out):
    for k in range(2):
        resid_out[k * half : (k + 1) * half] = scores[G + k, 0:half]
    for k in range(K):
        token_out[k * L : (k + 1) * L] = scores[G + 2 + k, :]
    for g in range(G):
        neuron_out[g * L : (g + 1) * L] = scores[g, :]


def shards(grad_out, resid_in, down_weight, hidden_clean, hidden_corrupt, patched):
    S = lax.axis_size("seq")
    T = lax.axis_size("tp")
    rows, width = grad_out.shape
    units, local_len = hidden_clean.shape
    L = math.gcd(units, 128)
    G = units // L
    C = max(c for c in range(1, 9) if G % c == 0)
    lanes = math.gcd(patched.shape[0], 1024)
    half = rows // 2
    scales = (
        1.0 / math.sqrt(width * T),
        1.0 / math.sqrt(patched.shape[0]),
        1.0 / math.sqrt(local_len * T),
    )
    dma = lambda *shape: pltpu.SemaphoreType.DMA(shape)
    K = local_len // L
    scores = pl.pallas_call(
        functools.partial(kernel, S, T, C, G, L, scales),
        out_shape=jax.ShapeDtypeStruct((G + 2 + K, L), F32),
        in_specs=[pl.BlockSpec(memory_space=pl.ANY)] * 6,
        out_specs=pl.BlockSpec(memory_space=pltpu.VMEM),
        scratch_shapes=[
            pltpu.VMEM((rows, width), BF16),
            pltpu.VMEM((rows, width), BF16),
            pltpu.VMEM((units, width), BF16),
            pltpu.VMEM((units, local_len), BF16),
            pltpu.VMEM((units, local_len), BF16),
            pltpu.VMEM((patched.shape[0] // lanes, 1, lanes), jnp.int32),
            pltpu.VMEM((rows, width), BF16),
            pltpu.VMEM((half, width), BF16),
            pltpu.VMEM((S // 2, rows, width), BF16),
            pltpu.VMEM((T, units, local_len), BF16),
            pltpu.VMEM((T, units, local_len), F32),
            pltpu.VMEM((units, local_len), BF16),
            pltpu.VMEM((units, local_len), BF16),
            pltpu.VMEM((units, 128), F32),
            pltpu.VMEM((units, 128), F32),
            pltpu.VMEM((T, 1, local_len), F32),
            pltpu.VMEM((T, 1, local_len), F32),
            pltpu.VMEM((1, local_len), F32),
            pltpu.VMEM((S, 1, local_len), F32),
            pltpu.VMEM((G + 2, L), F32),
            pltpu.VMEM((T, G + 2, L), F32),
            pltpu.VMEM((G, L), F32),
            pltpu.VMEM((2, 1, half), F32),
            pltpu.VMEM((1, half), F32),
            dma(4 + patched.shape[0] // lanes), dma(C), dma(4), dma(4), dma(S // 4, 2), dma(S // 4, 2), dma(S // 2, 2),
            dma(2, T, C), dma(T, C), dma(C), dma(C),
            dma(T), dma(T), dma(T), dma(T), dma(S), dma(S),
        ],
        compiler_params=pltpu.CompilerParams(
            collective_id=0, has_side_effects=True, vmem_limit_bytes=56 * 1024 * 1024
        ),
    )(
        grad_out, resid_in, down_weight, hidden_clean, hidden_corrupt,
        patched,
    )
    return pl.pallas_call(
        functools.partial(write, G, K, L, half),
        out_shape=(
            jax.ShapeDtypeStruct((rows,), F32),
            jax.ShapeDtypeStruct((local_len,), F32),
            jax.ShapeDtypeStruct((units,), F32),
        ),
        in_specs=[pl.BlockSpec(memory_space=pltpu.VMEM)],
        out_specs=[pl.BlockSpec(memory_space=pltpu.VMEM)] * 3,
    )(scores)


def solution(mesh):
    in_specs = (P("seq", "tp"), P("seq", "tp"), P("seq", "tp"), P("seq", "tp"), P("seq", "tp"), P())
    out_specs = (P("seq"), P("tp"), P("seq"))
    return jax.shard_map(shards, mesh=mesh, in_specs=in_specs, out_specs=out_specs, check_vma=False)
```

```python
import functools
import math

import jax
import jax.numpy as jnp
from jax import lax
from jax.experimental import pallas as pl
from jax.experimental.pallas import tpu as pltpu
from jax.sharding import PartitionSpec as P

F32 = jnp.float32
BF16 = jnp.bfloat16
NT = (((1,), (1,)), ((), ()))


def each(count, body):
    def step(index, carry):
        body(index)
        return carry

    lax.fori_loop(0, count, step, 0)


def kernel(
    S, T, C, G, L, scales,
    grad_hbm, resid_hbm, weight_hbm, clean_hbm, corrupt_hbm, patched_hbm,
    scores,
    grad, resid, weight, clean, corrupt, patched,
    partner_grad, partner_resid, means, diff, unit, partial, partial_in, mask, acc, token, token_in, token_sum,
    total_in, message, message_in, counts, scored, score_out,
    load_sem, weight_sem, pair_send, pair_recv, outer_send, inner_send, mean_recv, diff_send, diff_recv,
    part_send, part_recv, msg_send, msg_recv, tok_send, tok_recv, sum_send, sum_recv,
):
    seq = lax.axis_index("seq")
    tp = lax.axis_index("tp")
    pairs = S // 2
    partner = lax.rem(seq + pairs, S)
    upper = seq // pairs
    rows = grad.shape[0]
    half = rows // 2
    units = weight.shape[0]
    piece = units // C
    local_len = diff.shape[2]

    lanes = patched.shape[2]

    def local(source, target, index):
        return pltpu.make_async_copy(source, target, load_sem.at[index])

    loads = [
        local(clean_hbm, clean, 0),
        local(corrupt_hbm, corrupt, 1),
        local(grad_hbm, grad, 2),
        local(resid_hbm, resid, 3),
    ]
    for index in (2, 0, 1, 3):
        loads[index].start()

    def ids_load(k):
        return local(patched_hbm.at[pl.ds(pl.multiple_of(k * lanes, lanes), lanes)], patched.at[k, 0], 4 + k)

    each(patched.shape[0], lambda k: ids_load(k).start())

    def piece_rows(c):
        return pl.ds(pl.multiple_of(c * piece, 16), piece)

    def weight_load(c):
        return pltpu.make_async_copy(
            weight_hbm.at[piece_rows(c)], weight.at[piece_rows(c)], weight_sem.at[c]
        )

    def remote(source, target, send, recv, device):
        return pltpu.make_async_remote_copy(
            src_ref=source, dst_ref=target, send_sem=send, recv_sem=recv,
            device_id=device, device_id_type=pl.DeviceIdType.MESH,
        )

    barrier = pltpu.get_barrier_semaphore()

    def greet_seq(i):
        pl.semaphore_signal(
            barrier, inc=1, device_id=(lax.rem(seq + i + 1, S), tp),
            device_id_type=pl.DeviceIdType.MESH,
        )

    def greet_tp(i):
        pl.semaphore_signal(
            barrier, inc=1, device_id=(seq, lax.rem(tp + i + 1, T)),
            device_id_type=pl.DeviceIdType.MESH,
        )

    each(S - 1, greet_seq)
    each(T - 1, greet_tp)
    loads[2].wait()
    pl.semaphore_wait(barrier, S - 1 + T - 1)
    keep = pl.ds(pl.multiple_of(upper * half, 8), half)
    give = pl.ds(pl.multiple_of((1 - upper) * half, 8), half)

    def grad_copy(h):
        r = pl.ds(h * half, half)
        return remote(
            grad.at[r], partner_grad.at[r], pair_send.at[h], pair_recv.at[h], (partner, tp)
        )

    resid_copy = remote(
        resid.at[give], partner_resid, pair_send.at[2], pair_recv.at[2], (partner, tp)
    )
    score_copy = remote(
        score_out, scored.at[upper], pair_send.at[3], pair_recv.at[3], (partner, tp)
    )
    grad_copy(0).start()
    grad_copy(1).start()

    def diff_copy(block, c, step):
        place = diff.at[block, piece_rows(c)]
        direction = (step + 1) // 2
        return remote(
            place, place, diff_send.at[direction, block, c], diff_recv.at[block, c],
            (seq, tp + step),
        )

    def forward(block, c, step):
        @pl.when((tp + step >= 0) & (tp + step < T))
        def _():
            diff_copy(block, c, step).start()

    def own(c):
        forward(tp, c, 1)
        forward(tp, c, -1)

    loads[0].wait()
    loads[1].wait()

    def subtract(c):
        r = piece_rows(c)
        diff[tp, r, :] = (clean[r, :].astype(F32) - corrupt[r, :].astype(F32)).astype(BF16)
        own(c)

    each(C, subtract)

    def relay(s, c):
        @pl.when(tp - s >= 0)
        def _():
            diff_copy(tp - s, c, 1).wait_recv()
            if s + 1 <= T - 2:
                forward(tp - s, c, 1)

        @pl.when(tp + s < T)
        def _():
            diff_copy(tp + s, c, -1).wait_recv()
            if s + 1 <= T - 2:
                forward(tp + s, c, -1)

    each(C, lambda c: weight_load(c).start())

    outer = pairs // 2
    mine = lax.rem(seq, pairs)
    chip = mine // 2
    core = lax.rem(mine, 2)

    def mean_copy(block, h, send, target):
        place = means.at[block, pl.ds(h * half, half)]
        return remote(place, place, send, mean_recv.at[block, h], (upper * pairs + target, tp))

    def outer_copy(i, h):
        return mean_copy(mine, h, outer_send.at[i, h], lax.rem(chip + i, outer) * 2 + core)

    def inner_copy(i, h):
        block = lax.rem(chip + i, outer) * 2 + core
        return mean_copy(block, h, inner_send.at[i, h], chip * 2 + 1 - core)

    def await_mean(block, h):
        mean_copy(block, h, inner_send.at[0, h], chip * 2 + 1 - core).wait_recv()

    for h in range(2):
        grad_copy(h).wait()
        r = pl.ds(h * half, half)
        both = grad[r, :].astype(F32) + partner_grad[r, :].astype(F32)
        means[mine, r, :] = (both * 0.5).astype(BF16)
        each(outer - 1, lambda i: outer_copy(i + 1, h).start())
        inner_copy(0, h).start()
    loads[3].wait()
    resid_copy.start()

    each(patched.shape[0], lambda k: ids_load(k).wait())
    counts[...] = jnp.zeros_like(counts)
    group_ids = lax.broadcasted_iota(jnp.int32, (G, lanes), 0)
    lane_ids = lax.broadcasted_iota(jnp.int32, (L, lanes), 0)

    def count(k):
        ids = patched[k] - seq * units + S * units
        high = ids // L - (S * units) // L
        low = lax.rem(ids, L)
        counts[...] += lax.dot_general(
            jnp.where(high == group_ids, 1.0, 0.0).astype(BF16),
            jnp.where(low == lane_ids, 1.0, 0.0).astype(BF16),
            NT, preferred_element_type=F32,
        )

    each(patched.shape[0], count)

    def spread(g):
        row = jnp.broadcast_to(counts[pl.ds(g, 1), :], (128, L))
        mask[pl.ds(pl.multiple_of(g * L, 8), L), :] = row.T

    each(G, spread)
    acc[...] = jnp.zeros_like(acc)
    token[...] = jnp.zeros_like(token)

    each(C // 2, lambda c: relay(1, c))
    for h in range(2):

        def pass_on(i):
            await_mean(lax.rem(chip + i + 1, outer) * 2 + core, h)
            inner_copy(i + 1, h).start()

        each(outer - 1, pass_on)
    for h in range(2):
        each(outer, lambda i: await_mean(lax.rem(chip + i, outer) * 2 + 1 - core, h))

    blocks = T // 2
    at_end = (tp == 0) | (tp == T - 1)
    far = jnp.where(tp == 0, T - 1, 0)
    inward = jnp.where(tp == 0, 1, -1)

    def partial_copy(c):
        r = piece_rows(c)
        return remote(
            partial.at[r], partial_in.at[r], part_send.at[c], part_recv.at[c], (seq, tp + inward)
        )

    def multiply(side, c):
        r = piece_rows(c)
        right = means[pl.ds(side * outer, outer)]
        right = right.reshape(outer * rows, right.shape[-1])
        result = lax.dot_general(weight[r, :], right, NT, preferred_element_type=F32)
        for k in range(blocks):
            unit[side * blocks + k, r, :] = result[:, k * local_len : (k + 1) * local_len]

    far_side = 1 - tp // blocks

    def multiply_far(c):
        weight_load(c).wait()
        multiply(far_side, c)

        @pl.when(at_end)
        def _():
            r = piece_rows(c)
            partial[r, :] = unit[far, r, :].astype(BF16)
            partial_copy(c).start()

    each(C // 2, multiply_far)

    def multiply_and_relay(c):
        multiply_far(c + C // 2)
        relay(1, c + C // 2)

    each(C - C // 2, multiply_and_relay)
    each(C, lambda c: multiply(1 - far_side, c))

    def product(block, c):
        r = piece_rows(c)
        value = diff[block, r, :].astype(F32) * unit[block, r, :]
        masks = mask[r, :]
        for k in range(local_len // 128):
            part = value[:, k * 128 : (k + 1) * 128]
            acc[r, :] += part
            token[block, :, k * 128 : (k + 1) * 128] += jnp.sum(
                part * masks, axis=0, keepdims=True
            )

    def products(s, c):
        if s == 0:
            product(tp, c)
            return

        @pl.when(tp - s >= 0)
        def _():
            product(tp - s, c)

        @pl.when(tp + s < T)
        def _():
            product(tp + s, c)

    resid_copy.wait()
    sign = (1 - 2 * upper).astype(F32)

    difference = sign * (resid[keep, :].astype(F32) - partner_resid[...].astype(F32))

    def score(gradient):
        terms = difference * gradient.astype(F32)
        folded = terms[:, 0:128]
        for j in range(1, terms.shape[1] // 128):
            folded = folded + terms[:, j * 128 : (j + 1) * 128]
        return jnp.sum(folded.T, axis=0, keepdims=True)

    score_out[...] = score(partner_grad[keep, :])
    score_copy.start()
    scored[upper] = score(grad[keep, :])
    each(C, lambda c: products(0, c))
    each(C, lambda c: products(1, c))
    helped = ((tp == 1) | (tp == T - 2)) & (T > 2)
    helped_block = jnp.where(tp == 1, T - 1, 0)

    def help_in(c):
        @pl.when(helped)
        def _():
            r = piece_rows(c)
            remote(
                partial.at[r], partial_in.at[r], part_send.at[c], part_recv.at[c],
                (seq, jnp.where(tp == 1, 0, T - 1)),
            ).wait_recv()
            unit[helped_block, r, :] += partial_in[r, :].astype(F32)

    def fold(g):
        block = acc[pl.ds(pl.multiple_of(g * L, 8), L), :]
        message[pl.ds(g, 1), :] = jnp.sum(block.T, axis=0, keepdims=True)

    score_copy.wait()
    message[G:, :] = jnp.zeros((2, L), F32)
    for k in range(2):
        message[G + k : G + k + 1, 0:half] = scored[k]

    for s in range(2, T - 1):

        def last(c):
            relay(s, c)
            if s == T - 2:
                help_in(c)
            products(s, c)
            if s == T - 2:
                each(G // C, lambda g: fold(c * (G // C) + g))

        each(C, last)
    def token_copy(i):
        target = lax.rem(tp + i, T)
        return remote(
            token.at[target], token_in.at[tp], tok_send.at[i], tok_recv.at[tp], (seq, target)
        )

    each(T - 1, lambda i: token_copy(i + 1).start())

    def message_copy(i):
        return remote(
            message, message_in.at[tp], msg_send.at[i], msg_recv.at[tp],
            (seq, lax.rem(tp + i, T)),
        )

    each(T - 1, lambda i: message_copy(i + 1).start())

    token_in[tp] = token[tp]
    for h in range(2):
        each(outer - 1, lambda i: outer_copy(i + 1, h).wait_send())
        each(outer, lambda i: inner_copy(i, h).wait_send())

    def drain(c):
        def sent(block, step):
            @pl.when((tp + step >= 0) & (tp + step < T) & (block >= 0) & (block < T))
            def _():
                diff_copy(block, c, step).wait_send()

        for s in range(T - 2):
            sent(tp - s, 1)
            sent(tp + s, -1)

    each(C, drain)

    @pl.when(at_end)
    def _():
        each(C, lambda c: partial_copy(c).wait_send())

    def await_token(i):
        source = lax.rem(tp + i + 1, T)
        remote(
            token.at[0], token_in.at[source], tok_send.at[0], tok_recv.at[source], (seq, source)
        ).wait_recv()

    each(T - 1, await_token)
    token_sum[...] = jnp.sum(token_in[...], axis=0)

    def sum_copy(i):
        return remote(
            token_sum, total_in.at[seq], sum_send.at[i], sum_recv.at[seq],
            (lax.rem(seq + i, S), tp),
        )

    each(S - 1, lambda i: sum_copy(i + 1).start())
    total_in[seq] = token_sum[...]
    message_in[tp] = message[...]

    def await_message(i):
        source = lax.rem(tp + i + 1, T)
        remote(
            message, message_in.at[source], msg_send.at[0], msg_recv.at[source], (seq, source)
        ).wait_recv()

    each(T - 1, await_message)
    total = jnp.sum(message_in[...], axis=0)
    scores[0:G, :] = total[:G] * scales[2]
    scores[G : G + 2, :] = total[G:] * scales[0]

    def await_sum(i):
        source = lax.rem(seq + i + 1, S)
        remote(
            token_sum, total_in.at[source], sum_send.at[0], sum_recv.at[source], (source, tp)
        ).wait_recv()

    each(S - 1, await_sum)
    token_total = jnp.sum(total_in[...], axis=0) * scales[1]
    for k in range(local_len // L):
        scores[G + 2 + k : G + 3 + k, :] = token_total[:, k * L : (k + 1) * L]

    each(T - 1, lambda i: token_copy(i + 1).wait_send())
    each(T - 1, lambda i: message_copy(i + 1).wait_send())
    each(S - 1, lambda i: sum_copy(i + 1).wait_send())


def write(G, K, L, half, scores, resid_out, token_out, neuron_out):
    for k in range(2):
        resid_out[k * half : (k + 1) * half] = scores[G + k, 0:half]
    for k in range(K):
        token_out[k * L : (k + 1) * L] = scores[G + 2 + k, :]
    for g in range(G):
        neuron_out[g * L : (g + 1) * L] = scores[g, :]


def shards(grad_out, resid_in, down_weight, hidden_clean, hidden_corrupt, patched):
    S = lax.axis_size("seq")
    T = lax.axis_size("tp")
    rows, width = grad_out.shape
    units, local_len = hidden_clean.shape
    L = math.gcd(units, 128)
    G = units // L
    C = max(c for c in range(1, 9) if G % c == 0)
    lanes = math.gcd(patched.shape[0], 1024)
    half = rows // 2
    scales = (
        1.0 / math.sqrt(width * T),
        1.0 / math.sqrt(patched.shape[0]),
        1.0 / math.sqrt(local_len * T),
    )
    dma = lambda *shape: pltpu.SemaphoreType.DMA(shape)
    K = local_len // L
    scores = pl.pallas_call(
        functools.partial(kernel, S, T, C, G, L, scales),
        out_shape=jax.ShapeDtypeStruct((G + 2 + K, L), F32),
        in_specs=[pl.BlockSpec(memory_space=pl.ANY)] * 6,
        out_specs=pl.BlockSpec(memory_space=pltpu.VMEM),
        scratch_shapes=[
            pltpu.VMEM((rows, width), BF16),
            pltpu.VMEM((rows, width), BF16),
            pltpu.VMEM((units, width), BF16),
            pltpu.VMEM((units, local_len), BF16),
            pltpu.VMEM((units, local_len), BF16),
            pltpu.VMEM((patched.shape[0] // lanes, 1, lanes), jnp.int32),
            pltpu.VMEM((rows, width), BF16),
            pltpu.VMEM((half, width), BF16),
            pltpu.VMEM((S // 2, rows, width), BF16),
            pltpu.VMEM((T, units, local_len), BF16),
            pltpu.VMEM((T, units, local_len), F32),
            pltpu.VMEM((units, local_len), BF16),
            pltpu.VMEM((units, local_len), BF16),
            pltpu.VMEM((units, 128), F32),
            pltpu.VMEM((units, 128), F32),
            pltpu.VMEM((T, 1, local_len), F32),
            pltpu.VMEM((T, 1, local_len), F32),
            pltpu.VMEM((1, local_len), F32),
            pltpu.VMEM((S, 1, local_len), F32),
            pltpu.VMEM((G + 2, L), F32),
            pltpu.VMEM((T, G + 2, L), F32),
            pltpu.VMEM((G, L), F32),
            pltpu.VMEM((2, 1, half), F32),
            pltpu.VMEM((1, half), F32),
            dma(4 + patched.shape[0] // lanes), dma(C), dma(4), dma(4), dma(S // 4, 2), dma(S // 4, 2), dma(S // 2, 2),
            dma(2, T, C), dma(T, C), dma(C), dma(C),
            dma(T), dma(T), dma(T), dma(T), dma(S), dma(S),
        ],
        compiler_params=pltpu.CompilerParams(
            collective_id=0, has_side_effects=True, vmem_limit_bytes=56 * 1024 * 1024
        ),
    )(
        grad_out, resid_in, down_weight, hidden_clean, hidden_corrupt,
        patched,
    )
    return pl.pallas_call(
        functools.partial(write, G, K, L, half),
        out_shape=(
            jax.ShapeDtypeStruct((rows,), F32),
            jax.ShapeDtypeStruct((local_len,), F32),
            jax.ShapeDtypeStruct((units,), F32),
        ),
        in_specs=[pl.BlockSpec(memory_space=pltpu.VMEM)],
        out_specs=[pl.BlockSpec(memory_space=pltpu.VMEM)] * 3,
    )(scores)


def solution(mesh):
    in_specs = (P("seq", "tp"), P("seq", "tp"), P("seq", "tp"), P("seq", "tp"), P("seq", "tp"), P())
    out_specs = (P("seq"), P("tp"), P("seq"))
    return jax.shard_map(shards, mesh=mesh, in_specs=in_specs, out_specs=out_specs, check_vma=False)
```
